32 devices in a mesh: gz: 8 (over z, x), gy: 4 (over y, core).
Axes of the slice: x: 2, y: 2, z: 4, core: 2. Of those that a mesh axis runs over, the one named last changes fastest.
Arguments:
- features: bfloat16 [8, 4, 1, 64, 512], P('gz', 'gy'), may hold values from -6 to 6
- cotangent: bfloat16 [8, 4, 1, 64, 512], P('gz', 'gy'), may hold values from -6 to 6
- first_weight: bfloat16 [64, 1728], replicated, may hold values from -0.15625 to 0.15625
- second_weight: bfloat16 [64, 1728], replicated, may hold values from -0.15625 to 0.15625
- positions: int32 [8, 4, 1], P('gz', 'gy'), may hold values from 0 to 3, as said below
- counts: int32 [8, 4], P('gz', 'gy'), may hold values from 1 to 1, as said below
Outputs:
- output: bfloat16 [8, 4, 1, 64, 512], P('gz', 'gy')
- input_grad: bfloat16 [8, 4, 1, 64, 512], P('gz', 'gy')
- first_grad: float32 [64, 1728], replicated
- second_grad: float32 [64, 1728], replicated
The draws below stay inside these ranges and needn't reach their ends.
Inputs may be any that keep to these rules, and one draw needn't show every extreme that they name: The first counts[i, j] positions of each device are distinct. `counts`: some device has all 1 slots active.
All inputs are finite; a program needn't handle non-finite values.
Results may differ from the reference program's by a relative error of at most 0.0052.
Values may be sent and summed in bfloat16 or wider, within the bound.
A program may use at most 64 MiB of HBM per device.

```python
import math
import jax
import jax.numpy as jnp
from jax import lax

C = 64
E = 8
BY = 2
BX = 2
SLOTS = 1
CELLS = 16384
N_GZ = 8
N_GY = 4


def draw_positions(key, part):
    keys = jax.random.split(key, N_GZ * N_GY)
    orders = jax.vmap(lambda single: jax.random.permutation(single, BY * BX))(keys)
    return orders[:, :SLOTS].reshape(N_GZ, N_GY, SLOTS).astype(jnp.int32)


def draw_counts(key, part):
    base = jax.random.randint(jax.random.fold_in(key, 3), (N_GZ * N_GY,), 0, SLOTS)
    number = 1 + base * (base + 1) // SLOTS
    chosen = jax.random.randint(jax.random.fold_in(key, 7), (), 0, N_GZ * N_GY)
    number = jnp.where(jnp.arange(N_GZ * N_GY) == chosen, SLOTS, number)
    return number.reshape(N_GZ, N_GY).astype(jnp.int32)


def block_scale(own_key, extent, cuts, least, top_value):
    gain, own = 1.0, jax.random.fold_in(own_key, 6)
    for axis_at, blocks in cuts:
        steps = jnp.exp(jax.random.uniform(jax.random.fold_in(own, axis_at), (blocks,), jnp.float32, least / len(cuts), top_value / len(cuts)))
        gain = gain * jnp.repeat(steps, extent[axis_at] // blocks).reshape([-1 if axis == axis_at else 1 for axis in range(len(extent))])
    return gain


def scatter_about(stream_key, dims, deviation, most, shards=(), held_as=jnp.bfloat16):
    array = deviation * jax.random.normal(stream_key, dims, jnp.float32)
    if shards:
        array = array * block_scale(stream_key, dims, shards, -0.22, 0.18)
    return jnp.clip(array, -most, most).astype(held_as)


def setup_inputs(seed: int = 0) -> dict:
    streams_of = jax.random.split(jax.random.key(seed), 7)
    return {
        "features": scatter_about(streams_of[0], (N_GZ, N_GY, SLOTS, C, E ** 3), 1.0, 6.0, ((0, 8), (1, 4))),
        "cotangent": scatter_about(streams_of[1], (N_GZ, N_GY, SLOTS, C, E ** 3), 1.0, 6.0, ((0, 8), (1, 4))),
        "first_weight": scatter_about(streams_of[2], (C, 27 * C), (27 * C) ** -0.5, 0.15625),
        "second_weight": scatter_about(streams_of[3], (C, 27 * C), (27 * C) ** -0.5, 0.15625),
        "positions": draw_positions(jax.random.fold_in(streams_of[6], 71), 0),
        "counts": draw_counts(jax.random.fold_in(streams_of[6], 71), 0),
    }


def silu_slope(value):
    sig = jax.nn.sigmoid(value)
    return sig * (1.0 + value * (1.0 - sig))

def to_slab(bricks, places, live):
    channels = bricks.shape[1]
    masked = jnp.where(live[:, None, None], bricks, jnp.zeros_like(bricks))
    grid = jnp.zeros((BY * BX, channels, E ** 3), bricks.dtype).at[places].set(masked)
    grid = grid.reshape(BY, BX, channels, E, E, E)
    return grid.transpose(2, 3, 0, 4, 1, 5).reshape(channels, E, BY * E, BX * E)

def patch_of(padded, place):
    channels = padded.shape[0]
    zero = jnp.zeros((), jnp.int32)
    row_y = (place // BX).astype(jnp.int32) * E
    row_x = (place % BX).astype(jnp.int32) * E
    cube = lax.dynamic_slice(padded, (zero, zero, row_y, row_x), (channels, E + 2, E + 2, E + 2))
    pieces = []
    for depth in range(3):
        for height in range(3):
            for across in range(3):
                pieces.append(cube[:, depth:depth + E, height:height + E, across:across + E].reshape(channels, E ** 3))
    return jnp.concatenate(pieces, axis=0)

def flip_weight(weight):
    channels = weight.shape[0]
    return weight.reshape(channels, 27, channels)[:, ::-1, :].transpose(2, 1, 0).reshape(channels, 27 * channels)

def convolve(padded, weight, places):

    def single(place):
        return jnp.dot(weight, patch_of(padded, place), preferred_element_type=jnp.float32)
    return lax.map(single, places)

def weight_terms(padded, grads, places):
    channels = grads.shape[1]

    def step(total, item):
        place, grad_here = item
        term = lax.dot_general(grad_here, patch_of(padded, place), (((1,), (1,)), ((), ())), preferred_element_type=jnp.float32)
        return (total + term, 0)
    total, unused = lax.scan(step, jnp.zeros((channels, 27 * channels), jnp.float32), (places, grads))
    return total

def reference(features, cotangent, first_weight, second_weight, positions, counts):
    live_all = lax.iota(jnp.int32, SLOTS)[None, None, :] < counts[:, :, None]
    scale = 1.0 / math.sqrt(CELLS)

    def padded_of(all_bricks, iz, iy):
        rows = []
        for dz in (-1, 0, 1):
            row = []
            for dy in (-1, 0, 1):
                jz = iz + dz
                jy = iy + dy
                inside = (jz >= 0) & (jz < N_GZ) & (jy >= 0) & (jy < N_GY)
                cz = jnp.clip(jz, 0, N_GZ - 1)
                cy = jnp.clip(jy, 0, N_GY - 1)
                slab = to_slab(all_bricks[cz, cy], positions[cz, cy], live_all[cz, cy])
                row.append(jnp.where(inside, slab, jnp.zeros_like(slab)))
            rows.append(jnp.concatenate(row, axis=2))
        big = jnp.concatenate(rows, axis=1)
        cut = big[:, E - 1:2 * E + 1, BY * E - 1:2 * BY * E + 1, :]
        return jnp.pad(cut, ((0, 0), (0, 0), (0, 0), (1, 1)))

    def over_devices(fn):
        index = jnp.arange(N_GZ * N_GY, dtype=jnp.int32)
        result = lax.map(lambda d: fn(d // N_GY, d % N_GY), index)
        return jax.tree.map(lambda a: a.reshape((N_GZ, N_GY) + a.shape[1:]), result)

    def first_pass(iz, iy):
        live_col = live_all[iz, iy][:, None, None]
        pre = jnp.where(live_col, convolve(padded_of(features, iz, iy), first_weight, positions[iz, iy]), 0.0)
        return (pre, jax.nn.silu(pre).astype(jnp.bfloat16))
    first_pre, first_act = over_devices(first_pass)

    def second_pass(iz, iy):
        live_col = live_all[iz, iy][:, None, None]
        summed = features[iz, iy].astype(jnp.float32) + convolve(padded_of(first_act, iz, iy), second_weight, positions[iz, iy])
        result = jnp.where(live_col, jax.nn.silu(summed), 0.0).astype(jnp.bfloat16)
        grad_here = jnp.where(live_col, cotangent[iz, iy].astype(jnp.float32) * silu_slope(summed), 0.0).astype(jnp.bfloat16)
        return (result, grad_here)
    output, grad_sum = over_devices(second_pass)
    second_flip = flip_weight(second_weight)
    first_flip = flip_weight(first_weight)

    def third_pass(iz, iy):
        live_col = live_all[iz, iy][:, None, None]
        spread = convolve(padded_of(grad_sum, iz, iy), second_flip, positions[iz, iy])
        total = weight_terms(padded_of(first_act, iz, iy), grad_sum[iz, iy], positions[iz, iy])
        pre_grad = jnp.where(live_col, spread * silu_slope(first_pre[iz, iy]), 0.0).astype(jnp.bfloat16)
        return (pre_grad, total)
    pre_grad, second_terms = over_devices(third_pass)

    def fourth_pass(iz, iy):
        live_col = live_all[iz, iy][:, None, None]
        spread = convolve(padded_of(pre_grad, iz, iy), first_flip, positions[iz, iy])
        total = weight_terms(padded_of(features, iz, iy), pre_grad[iz, iy], positions[iz, iy])
        grad_in = jnp.where(live_col, grad_sum[iz, iy].astype(jnp.float32) + spread, 0.0).astype(jnp.bfloat16)
        return (grad_in, total)
    input_grad, first_terms = over_devices(fourth_pass)
    first_grad = lax.optimization_barrier(jnp.sum(first_terms, axis=(0, 1))) * scale
    second_grad = lax.optimization_barrier(jnp.sum(second_terms, axis=(0, 1))) * scale
    return (output, input_grad, first_grad, second_grad)
```

```python
import functools
import math

import jax
import jax.numpy as jnp
from jax import lax
from jax.experimental import pallas as pl
from jax.experimental.pallas import tpu as pltpu
from jax.sharding import PartitionSpec as P

E = 8
VOX = E**3
CH = 64
BX = 2
MESH = pl.DeviceIdType.MESH
F32 = jnp.float32
BF16 = jnp.bfloat16
FACES = ((-1, 0), (1, 0), (0, -1), (0, 1))
EDGES = ((-1, -1), (-1, 1), (1, -1), (1, 1))
PAIR = 2
TILES = 7


def sigmoid(value):
    return 1.0 / (1.0 + jnp.exp(-value))


def kernel(
    n_gz, n_gy,
    place_ref, count_ref, x_ref, ct_ref, w1_ref, w2_ref,
    out_ref, gin_ref, g1_ref, g2_ref,
    qx, qa, qg, wt1, wt2, wf1, wf2, pre_s, gs_s, masks,
    hf_send, hf_recv, he_send, he_recv,
    t_send, t_recv, z_recv, gath,
    hf_ss, hf_rs, he_ss, he_rs, t_ss, t_rs, z_ss, z_rs, g_ss, g_rs,
):
    gz = lax.axis_index("gz")
    gy = lax.axis_index("gy")
    members = PAIR * n_gy
    groups = n_gz // PAIR
    mine = (gz % PAIR) * n_gy + gy
    group = gz // PAIR

    def exists(dz, dy):
        ok = None
        for pos, step, count in ((gz, dz, n_gz), (gy, dy, n_gy)):
            if step:
                here = pos + step >= 0 if step < 0 else pos + step < count
                ok = here if ok is None else jnp.logical_and(ok, here)
        return ok

    def member_id(index):
        return (group * PAIR + index // n_gy, index % n_gy)

    def group_id(index):
        return (index * PAIR + gz % PAIR, gy)

    hf_recv[...] = jnp.zeros_like(hf_recv)
    he_recv[...] = jnp.zeros_like(he_recv)
    barrier = pltpu.get_barrier_semaphore()
    total = jnp.int32(members - 1 + groups - 1)
    for dz, dy in FACES + EDGES:
        ok = exists(dz, dy)
        total = total + ok.astype(jnp.int32)

        @pl.when(ok)
        def _(dz=dz, dy=dy):
            pl.semaphore_signal(barrier, inc=1, device_id=(gz + dz, gy + dy), device_id_type=MESH)

    for r in range(1, members):
        pl.semaphore_signal(barrier, inc=1, device_id=member_id((mine + r) % members), device_id_type=MESH)
    for r in range(1, groups):
        pl.semaphore_signal(barrier, inc=1, device_id=group_id((group + r) % groups), device_id_type=MESH)

    place = jnp.full((E, 128), place_ref[0], jnp.int32).astype(F32)
    live = jnp.full((E, 128), count_ref[0], jnp.int32).astype(F32)
    live = jnp.where(live > 0.5, 1.0, 0.0)
    lane = lax.broadcasted_iota(jnp.int32, (E, 128), 1)
    row = lax.broadcasted_iota(jnp.int32, (E, 128), 0)
    low = lane < CH

    def dup_t(block):
        return jnp.concatenate([block, block], axis=0).T

    def alive(value):
        return (value.reshape(-1, E, 128) * live[None]).reshape(value.shape)

    def x3(value):
        left = pltpu.roll(value, 1, 1)
        right = pltpu.roll(value, E - 1, 1)
        first = jnp.where(low[None], left, value)
        return jnp.concatenate([first, right], axis=-1)

    def halo_copy(e, kind, index):
        offsets, sends, recvs, ss, rs, rows = (
            (FACES, hf_send, hf_recv, hf_ss, hf_rs, 80 if e == 0 else 64)
            if kind == 0
            else (EDGES, he_send, he_recv, he_ss, he_rs, 16)
        )
        dz, dy = offsets[index]
        slot = offsets.index((-dz, -dy))
        return pltpu.make_async_remote_copy(
            src_ref=sends.at[e, index, pl.ds(0, rows)],
            dst_ref=recvs.at[e, slot, pl.ds(0, rows)],
            send_sem=ss.at[e, index],
            recv_sem=rs.at[e, slot],
            device_id=(gz + dz, gy + dy),
            device_id_type=MESH,
        )

    def halo_send(e, value):
        cube = value.reshape(E, E, E, 128)
        for index, (dz, dy) in enumerate(FACES):
            face = cube[0 if dz < 0 else E - 1] if dz else cube[:, 0 if dy < 0 else E - 1]
            face = face.reshape(64, 128)
            hf_send[e, index, 0:64, :] = face.astype(BF16)
            if e == 0:
                hf_send[e, index, 64:80, :] = jnp.concatenate([place, place], axis=0).astype(BF16)
        for index, (dz, dy) in enumerate(EDGES):
            edge = cube[0 if dz < 0 else E - 1, 0 if dy < 0 else E - 1]
            he_send[e, index] = jnp.concatenate([edge, place], axis=0).astype(BF16)
        if e == 0:
            pl.semaphore_wait(barrier, total)
        for kind, offsets in ((0, FACES), (1, EDGES)):
            for index, (dz, dy) in enumerate(offsets):

                @pl.when(exists(dz, dy))
                def _(kind=kind, index=index):
                    halo_copy(e, kind, index).start()

    def halo_wait(e):
        for kind, offsets in ((0, FACES), (1, EDGES)):
            for index, (dz, dy) in enumerate(offsets):

                @pl.when(exists(dz, dy))
                def _(kind=kind, offsets=offsets, dz=dz, dy=dy):
                    halo_copy(e, kind, offsets.index((-dz, -dy))).wait_recv()

    def sends_done(e):
        for kind, offsets in ((0, FACES), (1, EDGES)):
            for index, (dz, dy) in enumerate(offsets):

                @pl.when(exists(dz, dy))
                def _(kind=kind, index=index):
                    halo_copy(e, kind, index).wait_send()

    target0 = jnp.where(jnp.logical_and(low, row == 0), -1.0, 0.0)
    target1 = jnp.where(low, jnp.where(row == E - 1, 1.0, 0.0), 99.0)

    def x_mask(delta):
        return jnp.concatenate(
            [jnp.where(delta == target0, 1.0, 0.0), jnp.where(delta == target1, 1.0, 0.0)], axis=-1
        )

    own_mask = x_mask(jnp.zeros((E, 128), F32))
    own_y = jnp.where(place >= 1.5, 1.0, 0.0)
    own_x = place - 2.0 * own_y

    def make_masks():
        def of(theirs):
            their_y = jnp.where(theirs >= 1.5, 1.0, 0.0)
            return their_y, x_mask(theirs - 2.0 * their_y - own_x)

        def chosen(which, mask):
            keep = jnp.where(which, 1.0, 0.0)
            return mask * jnp.concatenate([keep, keep], axis=-1)

        for s in range(2):
            their_y, mask = of(hf_recv[0, s, 64:80, :].astype(F32)[0:E])
            for n, step in enumerate((-1.0, 0.0, 1.0)):
                masks[3 * s + n] = chosen(their_y - own_y == step, mask)
        for t in range(2):
            dy = 2.0 * t - 1.0
            their_y, mask = of(hf_recv[0, 2 + t, 64:80, :].astype(F32)[0:E])
            masks[6 + t] = chosen(2.0 * dy + their_y - own_y == dy, mask)
            for s in range(2):
                their_y, mask = of(he_recv[0, 2 * s + t].astype(F32)[E : 2 * E])
                masks[8 + 2 * s + t] = chosen(2.0 * dy + their_y - own_y == dy, mask)

    def fill_inside(q, value):
        q[1 : E + 1, 1 : E + 1] = (x3(value.reshape(64, E, 128)) * own_mask[None]).reshape(E, E, E, 256)

    def fill_halo(e, q):
        for s in range(2):
            plane = s * (E + 1)
            spread = x3(hf_recv[e, s, 0:64, :].astype(F32).reshape(E, E, 128))
            q[plane, 1 : E + 1] = spread * masks[3 * s + 1][None]
            for t in range(2):
                edge = he_recv[e, 2 * s + t].astype(F32)[0:E]
                edge = x3(edge[None])[0] * masks[8 + 2 * s + t]
                near = spread[E - 1 if t == 0 else 0] * masks[3 * s + 2 * t]
                q[plane, t * (E + 1)] = edge + near
        for t in range(2):
            spread = x3(hf_recv[e, 2 + t, 0:64, :].astype(F32).reshape(E, E, 128))
            q[1 : E + 1, t * (E + 1)] = spread * masks[6 + t][None]

    def patch(q, k):
        return q[k // 3 : k // 3 + E, k % 3 : k % 3 + E].reshape(VOX, 256).astype(BF16)

    def conv(q, w):
        acc = None
        for k in range(9):
            part = jnp.dot(patch(q, k), w[192 * k : 192 * k + 256, :], preferred_element_type=F32)
            acc = part if acc is None else acc + part
        return acc

    def turn_weight(w_ref, wt):
        for t in range(13):
            wt[128 * t : 128 * t + 128, :] = dup_t(w_ref[:, 128 * t : 128 * t + 128].astype(F32)).astype(BF16)
        wt[1664:1728, :] = dup_t(w_ref[:, 1664:1728].astype(F32)).astype(BF16)
        wt[1728:1792, :] = jnp.zeros((64, 128), BF16)

    def flip_weight(w_ref, wf):
        low64 = lax.broadcasted_iota(jnp.int32, (64, 128), 1) < CH
        for t in range(13):
            tile = w_ref[:, 128 * t : 128 * t + 128].astype(F32)
            turned = pltpu.roll(tile, 64, 1)
            at = (26 - 2 * t) * 64
            wf[at : at + 64, :] = jnp.where(low64, tile, turned).astype(BF16)
            wf[at - 64 : at, :] = jnp.where(low64, turned, tile).astype(BF16)
        last = w_ref[:, 1664:1728].astype(F32)
        wf[0:64, :] = jnp.concatenate([last, last], axis=1).astype(BF16)
        wf[1728:1792, :] = jnp.zeros((64, 128), BF16)

    def terms(g, grads, q):
        turned = grads.T[0:CH].astype(BF16)

        def put(t, tile):
            for r in range(4):
                t_send[g, 2 * r + t // TILES, :, 128 * (t % TILES) : 128 * (t % TILES) + 128] = tile[
                    16 * r : 16 * r + 16
                ].astype(BF16)

        for m in range(5):
            even = jnp.dot(turned, patch(q, 2 * m), preferred_element_type=F32)
            put(3 * m, even[:, 0:128])
            if m == 4:
                put(3 * m + 1, even[:, 128:256])
            else:
                odd = jnp.dot(turned, patch(q, 2 * m + 1), preferred_element_type=F32)
                odd = pltpu.roll(odd, 64, 1)
                put(3 * m + 1, even[:, 128:256] + odd[:, 0:128])
                put(3 * m + 2, odd[:, 128:256])

    def t_copy(g, r):
        to = (mine + r) % members
        return pltpu.make_async_remote_copy(
            src_ref=t_send.at[g, to], dst_ref=t_recv.at[g, mine],
            send_sem=t_ss.at[g, r], recv_sem=t_rs.at[g, r],
            device_id=member_id(to), device_id_type=MESH,
        )

    def z_copy(g, r):
        return pltpu.make_async_remote_copy(
            src_ref=z_recv.at[g, group], dst_ref=z_recv.at[g, group],
            send_sem=z_ss.at[g, r], recv_sem=z_rs.at[g, r],
            device_id=group_id((group + r) % groups), device_id_type=MESH,
        )

    def g_copy(g, r):
        return pltpu.make_async_remote_copy(
            src_ref=gath.at[g, mine], dst_ref=gath.at[g, mine],
            send_sem=g_ss.at[g, r], recv_sem=g_rs.at[g, r],
            device_id=member_id((mine + r) % members), device_id_type=MESH,
        )

    def recv_of(buffer, g, slot, ss, rs, r):
        return pltpu.make_async_remote_copy(
            src_ref=buffer.at[g, slot], dst_ref=buffer.at[g, slot],
            send_sem=ss.at[g, r], recv_sem=rs.at[g, r],
            device_id=member_id((mine + 1) % members), device_id_type=MESH,
        )

    def add_up(buffer, g, count):
        acc = buffer[g, 0].astype(F32)
        for n in range(1, count):
            acc = acc + buffer[g, n].astype(F32)
        return acc.astype(BF16)

    def scatter_start(g):
        for r in range(1, members):
            t_copy(g, r).start()
        t_recv[g, mine] = t_send[g, mine]

    def exchange_start(g):
        for r in range(1, members):
            recv_of(t_recv, g, (mine + members - r) % members, t_ss, t_rs, r).wait_recv()
        z_recv[g, group] = add_up(t_recv, g, members)
        for r in range(1, groups):
            z_copy(g, r).start()

    def gather_start(g):
        for r in range(1, groups):
            recv_of(z_recv, g, (group + groups - r) % groups, z_ss, z_rs, r).wait_recv()
        gath[g, mine] = add_up(z_recv, g, groups)
        for r in range(1, members):
            g_copy(g, r).start()

    def gather_end(g, ref):
        for r in range(1, members):
            recv_of(gath, g, (mine + members - r) % members, g_ss, g_rs, r).wait_recv()
        for r in range(4):
            ref[16 * r : 16 * r + 16, 0:896] = gath[g, 2 * r]
            ref[16 * r : 16 * r + 16, 896:1728] = gath[g, 2 * r + 1][:, 0:832]
        for r in range(1, members):
            t_copy(g, r).wait_send()
            g_copy(g, r).wait_send()
        for r in range(1, groups):
            z_copy(g, r).wait_send()

    x = dup_t(x_ref[...].astype(F32))
    field = alive(x)
    halo_send(0, field)
    fill_inside(qx, field)
    turn_weight(w1_ref, wt1)
    halo_wait(0)
    make_masks()
    fill_halo(0, qx)
    pre = conv(qx, wt1)
    pre_s[...] = pre
    act = alive(pre * sigmoid(pre)).astype(BF16).astype(F32)

    halo_send(1, act)
    fill_inside(qa, act)
    turn_weight(w2_ref, wt2)
    ct = dup_t(ct_ref[...].astype(F32))
    halo_wait(1)
    fill_halo(1, qa)
    summed = dup_t(x_ref[...].astype(F32)) + conv(qa, wt2)
    sig = sigmoid(summed)
    gs = alive(ct * (sig * (1.0 + summed * (1.0 - sig)))).astype(BF16).astype(F32)

    halo_send(2, gs)
    gs_s[...] = gs
    terms(0, gs, qa)
    scatter_start(0)
    out_ref[...] = alive(summed * sig).T[0:CH].astype(BF16)
    fill_inside(qg, gs)
    flip_weight(w2_ref, wf2)
    halo_wait(2)
    fill_halo(2, qg)
    act_grad = conv(qg, wf2)
    pre = pre_s[...]
    sig = sigmoid(pre)
    pg = alive(act_grad * (sig * (1.0 + pre * (1.0 - sig)))).astype(BF16).astype(F32)

    halo_send(3, pg)
    terms(1, pg, qx)
    scatter_start(1)
    exchange_start(0)
    fill_inside(qg, pg)
    flip_weight(w1_ref, wf1)
    exchange_start(1)
    gather_start(0)
    halo_wait(3)
    fill_halo(3, qg)
    gin = alive(gs_s[...] + conv(qg, wf1))
    gather_start(1)
    gin_ref[...] = gin.T[0:CH].astype(BF16)
    gather_end(0, g2_ref)
    gather_end(1, g1_ref)
    for e in range(4):
        sends_done(e)


def body(features, cotangent, first_weight, second_weight, positions, counts):
    n_gz = lax.axis_size("gz")
    n_gy = lax.axis_size("gy")
    slots = features.shape[2]
    scale = 1.0 / math.sqrt(n_gz * n_gy * slots * VOX)
    members = PAIR * n_gy
    groups = n_gz // PAIR
    vmem = pl.BlockSpec(memory_space=pltpu.VMEM)
    smem = pl.BlockSpec(memory_space=pltpu.SMEM)
    dma = pltpu.SemaphoreType.DMA
    output, input_grad, first_sum, second_sum = pl.pallas_call(
        functools.partial(kernel, n_gz, n_gy),
        out_shape=(
            jax.ShapeDtypeStruct((CH, VOX), BF16),
            jax.ShapeDtypeStruct((CH, VOX), BF16),
            jax.ShapeDtypeStruct((CH, 27 * CH), BF16),
            jax.ShapeDtypeStruct((CH, 27 * CH), BF16),
        ),
        in_specs=[smem, smem, vmem, vmem, vmem, vmem],
        out_specs=(vmem,) * 4,
        scratch_shapes=[
            pltpu.VMEM((E + 2, E + 2, E, 256), F32),
            pltpu.VMEM((E + 2, E + 2, E, 256), F32),
            pltpu.VMEM((E + 2, E + 2, E, 256), F32),
            pltpu.VMEM((1792, 128), BF16),
            pltpu.VMEM((1792, 128), BF16),
            pltpu.VMEM((1792, 128), BF16),
            pltpu.VMEM((1792, 128), BF16),
            pltpu.VMEM((VOX, 128), F32),
            pltpu.VMEM((VOX, 128), F32),
            pltpu.VMEM((12, E, 256), F32),
            pltpu.VMEM((4, 4, 80, 128), BF16),
            pltpu.VMEM((4, 4, 80, 128), BF16),
            pltpu.VMEM((4, 4, 16, 128), BF16),
            pltpu.VMEM((4, 4, 16, 128), BF16),
            pltpu.VMEM((2, members, 16, 128 * TILES), BF16),
            pltpu.VMEM((2, members, 16, 128 * TILES), BF16),
            pltpu.VMEM((2, groups, 16, 128 * TILES), BF16),
            pltpu.VMEM((2, members, 16, 128 * TILES), BF16),
            dma((4, 4)), dma((4, 4)), dma((4, 4)), dma((4, 4)),
            dma((2, members)), dma((2, members)),
            dma((2, groups)), dma((2, groups)),
            dma((2, members)), dma((2, members)),
        ],
        compiler_params=pltpu.CompilerParams(collective_id=0, has_side_effects=True),
    )(
        positions.reshape(1), counts.reshape(1), features[0, 0, 0], cotangent[0, 0, 0],
        first_weight, second_weight,
    )
    first_grad = first_sum.astype(F32) * scale
    second_grad = second_sum.astype(F32) * scale
    return (output[None, None, None], input_grad[None, None, None], first_grad, second_grad)


def solution(mesh):
    return jax.shard_map(
        body,
        mesh=mesh,
        in_specs=(
            P("gz", "gy", None, None, None),
            P("gz", "gy", None, None, None),
            P(),
            P(),
            P("gz", "gy", None),
            P("gz", "gy"),
        ),
        out_specs=(P("gz", "gy", None, None, None), P("gz", "gy", None, None, None), P(), P()),
        check_vma=False,
    )
```

```python
import functools
import math

import jax
import jax.numpy as jnp
from jax import lax
from jax.experimental import pallas as pl
from jax.experimental.pallas import tpu as pltpu
from jax.sharding import PartitionSpec as P

E = 8
VOX = E**3
CH = 64
BX = 2
MESH = pl.DeviceIdType.MESH
F32 = jnp.float32
BF16 = jnp.bfloat16
FACES = ((-1, 0), (1, 0), (0, -1), (0, 1))
EDGES = ((-1, -1), (-1, 1), (1, -1), (1, 1))
PAIR = 2
TILES = 7
UNITS = ((0, 0, 896), (1, 0, 512), (1, 512, 896))


def sigmoid(value):
    return 1.0 / (1.0 + jnp.exp(-value))


def kernel(
    n_gz, n_gy,
    place_ref, count_ref, x_ref, ct_ref, w1_ref, w2_ref,
    out_ref, gin_ref, g1_ref, g2_ref,
    qx, qa, qg, qp, acc, wt1, wt2, wf1, wf2, pre_s, gs_s, masks,
    hf_send, hf_recv, he_send, he_recv,
    t_send, t_recv, z_recv, gath,
    hf_ss, hf_rs, he_ss, he_rs, t_ss, t_rs, z_ss, z_rs, g_ss, g_rs,
):
    gz = lax.axis_index("gz")
    gy = lax.axis_index("gy")
    members = PAIR * n_gy
    groups = n_gz // PAIR
    mine = (gz % PAIR) * n_gy + gy
    group = gz // PAIR

    def exists(dz, dy):
        ok = None
        for pos, step, count in ((gz, dz, n_gz), (gy, dy, n_gy)):
            if step:
                here = pos + step >= 0 if step < 0 else pos + step < count
                ok = here if ok is None else jnp.logical_and(ok, here)
        return ok

    def member_id(index):
        return (group * PAIR + index // n_gy, index % n_gy)

    def group_id(index):
        return (index * PAIR + gz % PAIR, gy)

    hf_recv[...] = jnp.zeros_like(hf_recv)
    he_recv[...] = jnp.zeros_like(he_recv)
    barrier = pltpu.get_barrier_semaphore()
    total = jnp.int32(members - 1 + groups - 1)
    for dz, dy in FACES + EDGES:
        ok = exists(dz, dy)
        total = total + ok.astype(jnp.int32)

        @pl.when(ok)
        def _(dz=dz, dy=dy):
            pl.semaphore_signal(barrier, inc=1, device_id=(gz + dz, gy + dy), device_id_type=MESH)

    for r in range(1, members):
        pl.semaphore_signal(barrier, inc=1, device_id=member_id((mine + r) % members), device_id_type=MESH)
    for r in range(1, groups):
        pl.semaphore_signal(barrier, inc=1, device_id=group_id((group + r) % groups), device_id_type=MESH)

    place = jnp.full((E, 128), place_ref[0], jnp.int32).astype(F32)
    live = jnp.full((E, 128), count_ref[0], jnp.int32).astype(F32)
    live = jnp.where(live > 0.5, 1.0, 0.0)
    lane = lax.broadcasted_iota(jnp.int32, (E, 128), 1)
    row = lax.broadcasted_iota(jnp.int32, (E, 128), 0)
    low = lane < CH

    def dup_t(block):
        return jnp.concatenate([block, block], axis=0).T

    def alive(value):
        return (value.reshape(-1, E, 128) * live[None]).reshape(value.shape)

    def x3(value):
        left = pltpu.roll(value, 1, 1)
        right = pltpu.roll(value, E - 1, 1)
        first = jnp.where(low[None], left, value)
        return jnp.concatenate([first, right], axis=-1)

    def halo_copy(e, kind, index):
        offsets, sends, recvs, ss, rs, rows = (
            (FACES, hf_send, hf_recv, hf_ss, hf_rs, 80 if e == 0 else 64)
            if kind == 0
            else (EDGES, he_send, he_recv, he_ss, he_rs, 16)
        )
        dz, dy = offsets[index]
        slot = offsets.index((-dz, -dy))
        return pltpu.make_async_remote_copy(
            src_ref=sends.at[e, index, pl.ds(0, rows)],
            dst_ref=recvs.at[e, slot, pl.ds(0, rows)],
            send_sem=ss.at[e, index],
            recv_sem=rs.at[e, slot],
            device_id=(gz + dz, gy + dy),
            device_id_type=MESH,
        )

    def halo_send(e, value):
        cube = value.reshape(E, E, E, 128)
        for index, (dz, dy) in enumerate(FACES):
            face = cube[0 if dz < 0 else E - 1] if dz else cube[:, 0 if dy < 0 else E - 1]
            face = face.reshape(64, 128)
            hf_send[e, index, 0:64, :] = face.astype(BF16)
            if e == 0:
                hf_send[e, index, 64:80, :] = jnp.concatenate([place, place], axis=0).astype(BF16)
        for index, (dz, dy) in enumerate(EDGES):
            edge = cube[0 if dz < 0 else E - 1, 0 if dy < 0 else E - 1]
            he_send[e, index] = jnp.concatenate([edge, place], axis=0).astype(BF16)
        if e == 0:
            pl.semaphore_wait(barrier, total)
        for kind, offsets in ((0, FACES), (1, EDGES)):
            for index, (dz, dy) in enumerate(offsets):

                @pl.when(exists(dz, dy))
                def _(kind=kind, index=index):
                    halo_copy(e, kind, index).start()

    def arrive(e, kind, offsets, index):
        dz, dy = offsets[index]

        @pl.when(exists(dz, dy))
        def _():
            halo_copy(e, kind, offsets.index((-dz, -dy))).wait_recv()

    def face_wait(e, indices):
        for index in indices:
            arrive(e, 0, FACES, index)

    def edge_wait(e):
        for index in range(4):
            arrive(e, 1, EDGES, index)

    def sends_done(e):
        for kind, offsets in ((0, FACES), (1, EDGES)):
            for index, (dz, dy) in enumerate(offsets):

                @pl.when(exists(dz, dy))
                def _(kind=kind, index=index):
                    halo_copy(e, kind, index).wait_send()

    target0 = jnp.where(jnp.logical_and(low, row == 0), -1.0, 0.0)
    target1 = jnp.where(low, jnp.where(row == E - 1, 1.0, 0.0), 99.0)

    def x_mask(delta):
        return jnp.concatenate(
            [jnp.where(delta == target0, 1.0, 0.0), jnp.where(delta == target1, 1.0, 0.0)], axis=-1
        )

    own_mask = x_mask(jnp.zeros((E, 128), F32))
    own_y = jnp.where(place >= 1.5, 1.0, 0.0)
    own_x = place - 2.0 * own_y

    def make_masks(part):
        def of(theirs):
            their_y = jnp.where(theirs >= 1.5, 1.0, 0.0)
            return their_y, x_mask(theirs - 2.0 * their_y - own_x)

        def chosen(which, mask):
            keep = jnp.where(which, 1.0, 0.0)
            return mask * jnp.concatenate([keep, keep], axis=-1)

        if part == 0:
            for s in range(2):
                their_y, mask = of(hf_recv[0, s, 64:80, :].astype(F32)[0:E])
                for n, step in enumerate((-1.0, 0.0, 1.0)):
                    masks[3 * s + n] = chosen(their_y - own_y == step, mask)
        for t in range(2):
            dy = 2.0 * t - 1.0
            if part == 1:
                their_y, mask = of(hf_recv[0, 2 + t, 64:80, :].astype(F32)[0:E])
                masks[6 + t] = chosen(2.0 * dy + their_y - own_y == dy, mask)
            if part == 2:
                for s in range(2):
                    their_y, mask = of(he_recv[0, 2 * s + t].astype(F32)[E : 2 * E])
                    masks[8 + 2 * s + t] = chosen(2.0 * dy + their_y - own_y == dy, mask)

    def fill_inside(q, value):
        q[1 : E + 1, 1 : E + 1] = (x3(value.reshape(64, E, 128)) * own_mask[None]).reshape(E, E, E, 256)

    def patch(q, k):
        return q[k // 3 : k // 3 + E, k % 3 : k % 3 + E].reshape(VOX, 256).astype(BF16)

    def clear_halo(q):
        for plane in (0, E + 1):
            q[plane] = jnp.zeros((E + 2, E, 256), F32)
            q[1 : E + 1, plane] = jnp.zeros((E, E, 256), F32)

    def rows_of(w, k):
        return w[192 * k : 192 * k + 256, :]

    def conv_inside(q, w):
        total = None
        for k in range(9):
            part = jnp.dot(patch(q, k), rows_of(w, k), preferred_element_type=F32)
            total = part if total is None else total + part
        acc[...] = total.reshape(E, E, E, 128)

    def conv_halo(e, q, w):
        def side(pieces):
            total = None
            for piece, k in pieces:
                part = jnp.dot(piece.reshape(64, 256).astype(BF16), rows_of(w, k), preferred_element_type=F32)
                total = part if total is None else total + part
            return total.reshape(E, E, 128)

        face_wait(e, (2, 3))
        if e == 0:
            make_masks(1)
        for t in range(2):
            spread = x3(hf_recv[e, 2 + t, 0:64, :].astype(F32).reshape(E, E, 128))
            q[1 : E + 1, t * (E + 1)] = spread * masks[6 + t][None]
            acc[:, t * (E - 1)] += side(
                [(q[dz : dz + E, t * (E + 1)], 3 * dz + 2 * t) for dz in range(3)]
            )
        face_wait(e, (0, 1))
        if e == 0:
            make_masks(0)
        for s in range(2):
            plane = s * (E + 1)
            spread = x3(hf_recv[e, s, 0:64, :].astype(F32).reshape(E, E, 128))
            q[plane, 1 : E + 1] = spread * masks[3 * s + 1][None]
            for t in range(2):
                q[plane, t * (E + 1)] = spread[E - 1 if t == 0 else 0] * masks[3 * s + 2 * t]
            acc[s * (E - 1)] += side([(q[plane, dy : dy + E], 6 * s + dy) for dy in range(3)])
        edge_wait(e)
        if e == 0:
            make_masks(2)
        for s in range(2):
            for t in range(2):
                edge = he_recv[e, 2 * s + t].astype(F32)[0:E]
                edge = x3(edge[None])[0] * masks[8 + 2 * s + t]
                q[s * (E + 1), t * (E + 1)] += edge
                acc[s * (E - 1), t * (E - 1)] += jnp.dot(
                    edge.astype(BF16), rows_of(w, 6 * s + 2 * t), preferred_element_type=F32
                )
        return acc[...].reshape(VOX, 128)

    def turn_weight(w_ref, wt):
        for t in range(13):
            wt[128 * t : 128 * t + 128, :] = dup_t(w_ref[:, 128 * t : 128 * t + 128].astype(F32)).astype(BF16)
        wt[1664:1728, :] = dup_t(w_ref[:, 1664:1728].astype(F32)).astype(BF16)
        wt[1728:1792, :] = jnp.zeros((64, 128), BF16)

    def flip_weight(w_ref, wf):
        low64 = lax.broadcasted_iota(jnp.int32, (64, 128), 1) < CH
        for t in range(13):
            tile = w_ref[:, 128 * t : 128 * t + 128].astype(F32)
            turned = pltpu.roll(tile, 64, 1)
            at = (26 - 2 * t) * 64
            wf[at : at + 64, :] = jnp.where(low64, tile, turned).astype(BF16)
            wf[at - 64 : at, :] = jnp.where(low64, turned, tile).astype(BF16)
        last = w_ref[:, 1664:1728].astype(F32)
        wf[0:64, :] = jnp.concatenate([last, last], axis=1).astype(BF16)
        wf[1728:1792, :] = jnp.zeros((64, 128), BF16)

    def terms(g, grads, q):
        turned = grads.T[0:CH].astype(BF16)

        def put(t, tile):
            for r in range(4):
                t_send[g, 2 * r + t // TILES, :, 128 * (t % TILES) : 128 * (t % TILES) + 128] = tile[
                    16 * r : 16 * r + 16
                ].astype(BF16)

        for m in range(5):
            even = jnp.dot(turned, patch(q, 2 * m), preferred_element_type=F32)
            put(3 * m, even[:, 0:128])
            if m == 4:
                put(3 * m + 1, even[:, 128:256])
            else:
                odd = jnp.dot(turned, patch(q, 2 * m + 1), preferred_element_type=F32)
                odd = pltpu.roll(odd, 64, 1)
                put(3 * m + 1, even[:, 128:256] + odd[:, 0:128])
                put(3 * m + 2, odd[:, 128:256])

    def part_of(buffer, u, slot):
        g, lo, hi = UNITS[u]
        return buffer.at[g, slot, :, lo:hi]

    def t_copy(u, r):
        to = (mine + r) % members
        return pltpu.make_async_remote_copy(
            src_ref=part_of(t_send, u, to), dst_ref=part_of(t_recv, u, mine),
            send_sem=t_ss.at[u, r], recv_sem=t_rs.at[u, r],
            device_id=member_id(to), device_id_type=MESH,
        )

    def z_copy(u, r):
        return pltpu.make_async_remote_copy(
            src_ref=part_of(z_recv, u, group), dst_ref=part_of(z_recv, u, group),
            send_sem=z_ss.at[u, r], recv_sem=z_rs.at[u, r],
            device_id=group_id((group + r) % groups), device_id_type=MESH,
        )

    def g_copy(u, r):
        return pltpu.make_async_remote_copy(
            src_ref=part_of(gath, u, mine), dst_ref=part_of(gath, u, mine),
            send_sem=g_ss.at[u, r], recv_sem=g_rs.at[u, r],
            device_id=member_id((mine + r) % members), device_id_type=MESH,
        )

    def recv_of(buffer, u, slot, ss, rs, r):
        return pltpu.make_async_remote_copy(
            src_ref=part_of(buffer, u, slot), dst_ref=part_of(buffer, u, slot),
            send_sem=ss.at[u, r], recv_sem=rs.at[u, r],
            device_id=member_id((mine + 1) % members), device_id_type=MESH,
        )

    def add_up(buffer, u, count):
        g, lo, hi = UNITS[u]
        total = buffer[g, 0, :, lo:hi].astype(F32)
        for n in range(1, count):
            total = total + buffer[g, n, :, lo:hi].astype(F32)
        return total.astype(BF16)

    def scatter_start(u):
        g, lo, hi = UNITS[u]
        for r in range(1, members):
            t_copy(u, r).start()
        t_recv[g, mine, :, lo:hi] = t_send[g, mine, :, lo:hi]

    def exchange_start(u):
        g, lo, hi = UNITS[u]
        for r in range(1, members):
            recv_of(t_recv, u, (mine + members - r) % members, t_ss, t_rs, r).wait_recv()
        z_recv[g, group, :, lo:hi] = add_up(t_recv, u, members)
        for r in range(1, groups):
            z_copy(u, r).start()

    def gather_start(u):
        g, lo, hi = UNITS[u]
        for r in range(1, groups):
            recv_of(z_recv, u, (group + groups - r) % groups, z_ss, z_rs, r).wait_recv()
        gath[g, mine, :, lo:hi] = add_up(z_recv, u, groups)
        for r in range(1, members):
            g_copy(u, r).start()

    def gather_end(u, ref):
        g, lo, hi = UNITS[u]
        for r in range(1, members):
            recv_of(gath, u, (mine + members - r) % members, g_ss, g_rs, r).wait_recv()
        for r in range(4):
            ref[16 * r : 16 * r + 16, lo:hi] = gath[g, 2 * r, :, lo:hi]
            end = min(hi, 832)
            ref[16 * r : 16 * r + 16, 896 + lo : 896 + end] = gath[g, 2 * r + 1, :, lo:end]

    def reduce_done(u):
        for r in range(1, members):
            t_copy(u, r).wait_send()
            g_copy(u, r).wait_send()
        for r in range(1, groups):
            z_copy(u, r).wait_send()

    x = dup_t(x_ref[...].astype(F32))
    field = alive(x)
    fill_inside(qx, field)
    for q in (qx, qa, qg, qp):
        clear_halo(q)
    turn_weight(w1_ref, wt1)
    halo_send(0, field)
    conv_inside(qx, wt1)
    turn_weight(w2_ref, wt2)
    flip_weight(w2_ref, wf2)
    pre = conv_halo(0, qx, wt1)
    act = alive(pre * sigmoid(pre)).astype(BF16).astype(F32)

    halo_send(1, act)
    pre_s[...] = pre
    fill_inside(qa, act)
    conv_inside(qa, wt2)
    flip_weight(w1_ref, wf1)
    ct = dup_t(ct_ref[...].astype(F32))
    summed = dup_t(x_ref[...].astype(F32)) + conv_halo(1, qa, wt2)
    sig = sigmoid(summed)
    gs = alive(ct * (sig * (1.0 + summed * (1.0 - sig)))).astype(BF16).astype(F32)

    halo_send(2, gs)
    gs_s[...] = gs
    terms(0, gs, qa)
    scatter_start(0)
    fill_inside(qg, gs)
    conv_inside(qg, wf2)
    out_ref[...] = alive(summed * sig).T[0:CH].astype(BF16)
    act_grad = conv_halo(2, qg, wf2)
    pre = pre_s[...]
    sig = sigmoid(pre)
    pg = alive(act_grad * (sig * (1.0 + pre * (1.0 - sig)))).astype(BF16).astype(F32)

    halo_send(3, pg)
    terms(1, pg, qx)
    scatter_start(1)
    scatter_start(2)
    exchange_start(0)
    fill_inside(qp, pg)
    conv_inside(qp, wf1)
    exchange_start(1)
    exchange_start(2)
    gather_start(0)
    gin = alive(gs_s[...] + conv_halo(3, qp, wf1))
    gather_start(1)
    gather_start(2)
    gin_ref[...] = gin.T[0:CH].astype(BF16)
    for e in range(4):
        sends_done(e)
    gather_end(0, g2_ref)
    gather_end(1, g1_ref)
    gather_end(2, g1_ref)
    for u in range(3):
        reduce_done(u)


def finish(scale, out_in, gin_in, g1_in, g2_in, out_ref, gin_ref, g1_ref, g2_ref):
    out_ref[...] = out_in[...]
    gin_ref[...] = gin_in[...]
    g1_ref[...] = g1_in[...].astype(F32) * scale
    g2_ref[...] = g2_in[...].astype(F32) * scale


def body(features, cotangent, first_weight, second_weight, positions, counts):
    n_gz = lax.axis_size("gz")
    n_gy = lax.axis_size("gy")
    slots = features.shape[2]
    scale = 1.0 / math.sqrt(n_gz * n_gy * slots * VOX)
    members = PAIR * n_gy
    groups = n_gz // PAIR
    vmem = pl.BlockSpec(memory_space=pltpu.VMEM)
    smem = pl.BlockSpec(memory_space=pltpu.SMEM)
    dma = pltpu.SemaphoreType.DMA
    output, input_grad, first_sum, second_sum = pl.pallas_call(
        functools.partial(kernel, n_gz, n_gy),
        out_shape=(
            jax.ShapeDtypeStruct((CH, VOX), BF16),
            jax.ShapeDtypeStruct((CH, VOX), BF16),
            jax.ShapeDtypeStruct((CH, 27 * CH), BF16),
            jax.ShapeDtypeStruct((CH, 27 * CH), BF16),
        ),
        in_specs=[smem, smem, vmem, vmem, vmem, vmem],
        out_specs=(vmem,) * 4,
        scratch_shapes=[
            pltpu.VMEM((E + 2, E + 2, E, 256), F32),
            pltpu.VMEM((E + 2, E + 2, E, 256), F32),
            pltpu.VMEM((E + 2, E + 2, E, 256), F32),
            pltpu.VMEM((E + 2, E + 2, E, 256), F32),
            pltpu.VMEM((E, E, E, 128), F32),
            pltpu.VMEM((1792, 128), BF16),
            pltpu.VMEM((1792, 128), BF16),
            pltpu.VMEM((1792, 128), BF16),
            pltpu.VMEM((1792, 128), BF16),
            pltpu.VMEM((VOX, 128), F32),
            pltpu.VMEM((VOX, 128), F32),
            pltpu.VMEM((12, E, 256), F32),
            pltpu.VMEM((4, 4, 80, 128), BF16),
            pltpu.VMEM((4, 4, 80, 128), BF16),
            pltpu.VMEM((4, 4, 16, 128), BF16),
            pltpu.VMEM((4, 4, 16, 128), BF16),
            pltpu.VMEM((2, members, 16, 128 * TILES), BF16),
            pltpu.VMEM((2, members, 16, 128 * TILES), BF16),
            pltpu.VMEM((2, groups, 16, 128 * TILES), BF16),
            pltpu.VMEM((2, members, 16, 128 * TILES), BF16),
            dma((4, 4)), dma((4, 4)), dma((4, 4)), dma((4, 4)),
            dma((3, members)), dma((3, members)),
            dma((3, groups)), dma((3, groups)),
            dma((3, members)), dma((3, members)),
        ],
        compiler_params=pltpu.CompilerParams(collective_id=0, has_side_effects=True),
    )(
        positions.reshape(1), counts.reshape(1), features[0, 0, 0], cotangent[0, 0, 0],
        first_weight, second_weight,
    )
    grad = jax.ShapeDtypeStruct((CH, 27 * CH), F32)
    brick = jax.ShapeDtypeStruct((CH, VOX), BF16)
    output, input_grad, first_grad, second_grad = pl.pallas_call(
        functools.partial(finish, scale),
        out_shape=(brick, brick, grad, grad),
        in_specs=[vmem] * 4,
        out_specs=(vmem,) * 4,
    )(output, input_grad, first_sum, second_sum)
    return (output[None, None, None], input_grad[None, None, None], first_grad, second_grad)


def solution(mesh):
    return jax.shard_map(
        body,
        mesh=mesh,
        in_specs=(
            P("gz", "gy", None, None, None),
            P("gz", "gy", None, None, None),
            P(),
            P(),
            P("gz", "gy", None),
            P("gz", "gy"),
        ),
        out_specs=(P("gz", "gy", None, None, None), P("gz", "gy", None, None, None), P(), P()),
        check_vma=False,
    )
```

```python
import functools
import math

import jax
import jax.numpy as jnp
from jax import lax
from jax.experimental import pallas as pl
from jax.experimental.pallas import tpu as pltpu
from jax.sharding import PartitionSpec as P

E = 8
VOX = E**3
CH = 64
BX = 2
MESH = pl.DeviceIdType.MESH
F32 = jnp.float32
BF16 = jnp.bfloat16
FACES = ((-1, 0), (1, 0), (0, -1), (0, 1))
EDGES = ((-1, -1), (-1, 1), (1, -1), (1, 1))
PAIR = 2
TILES = 7
UNITS = ((0, 0, 896), (1, 0, 512), (1, 512, 896))


def sigmoid(value):
    return 1.0 / (1.0 + jnp.exp(-value))


def kernel(
    n_gz, n_gy,
    place_ref, count_ref, x_hbm, ct_hbm, w1_hbm, w2_hbm,
    out_ref, gin_ref, g1_ref, g2_ref,
    x_ref, ct_ref, w1_ref, w2_ref, in_sems,
    qx, qa, qg, qp, acc, wt1, wt2, wf1, wf2, pre_s, gs_s, masks,
    hf_send, hf_recv, he_send, he_recv,
    t_send, t_recv, z_recv, gath,
    hf_ss, hf_rs, he_ss, he_rs, t_ss, t_rs, z_ss, z_rs, g_ss, g_rs,
):
    gz = lax.axis_index("gz")
    gy = lax.axis_index("gy")
    members = PAIR * n_gy
    groups = n_gz // PAIR
    mine = (gz % PAIR) * n_gy + gy
    group = gz // PAIR

    def exists(dz, dy):
        ok = None
        for pos, step, count in ((gz, dz, n_gz), (gy, dy, n_gy)):
            if step:
                here = pos + step >= 0 if step < 0 else pos + step < count
                ok = here if ok is None else jnp.logical_and(ok, here)
        return ok

    def member_id(index):
        return (group * PAIR + index // n_gy, index % n_gy)

    def group_id(index):
        return (index * PAIR + gz % PAIR, gy)

    hf_recv[...] = jnp.zeros_like(hf_recv)
    he_recv[...] = jnp.zeros_like(he_recv)
    barrier = pltpu.get_barrier_semaphore()
    total = jnp.int32(members - 1 + groups - 1)
    for dz, dy in FACES + EDGES:
        ok = exists(dz, dy)
        total = total + ok.astype(jnp.int32)

        @pl.when(ok)
        def _(dz=dz, dy=dy):
            pl.semaphore_signal(barrier, inc=1, device_id=(gz + dz, gy + dy), device_id_type=MESH)

    for r in range(1, members):
        pl.semaphore_signal(barrier, inc=1, device_id=member_id((mine + r) % members), device_id_type=MESH)
    for r in range(1, groups):
        pl.semaphore_signal(barrier, inc=1, device_id=group_id((group + r) % groups), device_id_type=MESH)

    loads = [
        pltpu.make_async_copy(src, dst, in_sems.at[n])
        for n, (src, dst) in enumerate(
            ((x_hbm, x_ref), (w1_hbm, w1_ref), (w2_hbm, w2_ref), (ct_hbm, ct_ref))
        )
    ]
    for load in loads:
        load.start()

    place = jnp.full((E, 128), place_ref[0], jnp.int32).astype(F32)
    live = jnp.full((E, 128), count_ref[0], jnp.int32).astype(F32)
    live = jnp.where(live > 0.5, 1.0, 0.0)
    lane = lax.broadcasted_iota(jnp.int32, (E, 128), 1)
    row = lax.broadcasted_iota(jnp.int32, (E, 128), 0)
    low = lane < CH

    def dup_t(block):
        return jnp.concatenate([block, block], axis=0).T

    def alive(value):
        return (value.reshape(-1, E, 128) * live[None]).reshape(value.shape)

    def x3(value):
        left = pltpu.roll(value, 1, 1)
        right = pltpu.roll(value, E - 1, 1)
        first = jnp.where(low[None], left, value)
        return jnp.concatenate([first, right], axis=-1)

    def halo_copy(e, kind, index):
        offsets, sends, recvs, ss, rs, rows = (
            (FACES, hf_send, hf_recv, hf_ss, hf_rs, 80 if e == 0 else 64)
            if kind == 0
            else (EDGES, he_send, he_recv, he_ss, he_rs, 16)
        )
        dz, dy = offsets[index]
        slot = offsets.index((-dz, -dy))
        return pltpu.make_async_remote_copy(
            src_ref=sends.at[e, index, pl.ds(0, rows)],
            dst_ref=recvs.at[e, slot, pl.ds(0, rows)],
            send_sem=ss.at[e, index],
            recv_sem=rs.at[e, slot],
            device_id=(gz + dz, gy + dy),
            device_id_type=MESH,
        )

    def halo_send(e, value):
        cube = value.reshape(E, E, E, 128)
        for index, (dz, dy) in enumerate(FACES):
            face = cube[0 if dz < 0 else E - 1] if dz else cube[:, 0 if dy < 0 else E - 1]
            face = face.reshape(64, 128)
            hf_send[e, index, 0:64, :] = face.astype(BF16)
            if e == 0:
                hf_send[e, index, 64:80, :] = jnp.concatenate([place, place], axis=0).astype(BF16)
        for index, (dz, dy) in enumerate(EDGES):
            edge = cube[0 if dz < 0 else E - 1, 0 if dy < 0 else E - 1]
            he_send[e, index] = jnp.concatenate([edge, place], axis=0).astype(BF16)
        if e == 0:
            pl.semaphore_wait(barrier, total)
        for kind, offsets in ((1, EDGES), (0, FACES)):
            for index, (dz, dy) in enumerate(offsets):

                @pl.when(exists(dz, dy))
                def _(kind=kind, index=index):
                    halo_copy(e, kind, index).start()

    def arrive(e, kind, offsets, index):
        dz, dy = offsets[index]

        @pl.when(exists(dz, dy))
        def _():
            halo_copy(e, kind, offsets.index((-dz, -dy))).wait_recv()

    def face_wait(e, indices):
        for index in indices:
            arrive(e, 0, FACES, index)

    def edge_wait(e):
        for index in range(4):
            arrive(e, 1, EDGES, index)

    def sends_done(e):
        for kind, offsets in ((0, FACES), (1, EDGES)):
            for index, (dz, dy) in enumerate(offsets):

                @pl.when(exists(dz, dy))
                def _(kind=kind, index=index):
                    halo_copy(e, kind, index).wait_send()

    target0 = jnp.where(jnp.logical_and(low, row == 0), -1.0, 0.0)
    target1 = jnp.where(low, jnp.where(row == E - 1, 1.0, 0.0), 99.0)

    def x_mask(delta):
        return jnp.concatenate(
            [jnp.where(delta == target0, 1.0, 0.0), jnp.where(delta == target1, 1.0, 0.0)], axis=-1
        )

    own_mask = x_mask(jnp.zeros((E, 128), F32))
    own_y = jnp.where(place >= 1.5, 1.0, 0.0)
    own_x = place - 2.0 * own_y

    def make_masks(part):
        def of(theirs):
            their_y = jnp.where(theirs >= 1.5, 1.0, 0.0)
            return their_y, x_mask(theirs - 2.0 * their_y - own_x)

        def chosen(which, mask):
            keep = jnp.where(which, 1.0, 0.0)
            return mask * jnp.concatenate([keep, keep], axis=-1)

        if part == 0:
            for s in range(2):
                their_y, mask = of(hf_recv[0, s, 64:80, :].astype(F32)[0:E])
                for n, step in enumerate((-1.0, 0.0, 1.0)):
                    masks[3 * s + n] = chosen(their_y - own_y == step, mask)
        for t in range(2):
            dy = 2.0 * t - 1.0
            if part == 1:
                their_y, mask = of(hf_recv[0, 2 + t, 64:80, :].astype(F32)[0:E])
                masks[6 + t] = chosen(2.0 * dy + their_y - own_y == dy, mask)
            if part == 2:
                for s in range(2):
                    their_y, mask = of(he_recv[0, 2 * s + t].astype(F32)[E : 2 * E])
                    masks[8 + 2 * s + t] = chosen(2.0 * dy + their_y - own_y == dy, mask)

    def fill_inside(q, value):
        q[1 : E + 1, 1 : E + 1] = (x3(value.reshape(64, E, 128)) * own_mask[None]).reshape(E, E, E, 256)

    def patch(q, k):
        return q[k // 3 : k // 3 + E, k % 3 : k % 3 + E].reshape(VOX, 256).astype(BF16)

    def clear_halo(q):
        for plane in (0, E + 1):
            q[plane] = jnp.zeros((E + 2, E, 256), F32)
            q[1 : E + 1, plane] = jnp.zeros((E, E, 256), F32)

    def rows_of(w, k):
        return w[192 * k : 192 * k + 256, :]

    def conv_inside(q, w):
        total = None
        for k in range(9):
            part = jnp.dot(patch(q, k), rows_of(w, k), preferred_element_type=F32)
            total = part if total is None else total + part
        acc[...] = total.reshape(E, E, E, 128)

    def conv_halo(e, q, w):
        def side(pieces):
            total = None
            for piece, k in pieces:
                part = jnp.dot(piece.reshape(64, 256).astype(BF16), rows_of(w, k), preferred_element_type=F32)
                total = part if total is None else total + part
            return total.reshape(E, E, 128)

        face_wait(e, (2, 3))
        if e == 0:
            make_masks(1)
        for t in range(2):
            spread = x3(hf_recv[e, 2 + t, 0:64, :].astype(F32).reshape(E, E, 128))
            q[1 : E + 1, t * (E + 1)] = spread * masks[6 + t][None]
            acc[:, t * (E - 1)] += side(
                [(q[dz : dz + E, t * (E + 1)], 3 * dz + 2 * t) for dz in range(3)]
            )
        face_wait(e, (0, 1))
        if e == 0:
            make_masks(0)
        for s in range(2):
            plane = s * (E + 1)
            spread = x3(hf_recv[e, s, 0:64, :].astype(F32).reshape(E, E, 128))
            q[plane, 1 : E + 1] = spread * masks[3 * s + 1][None]
            for t in range(2):
                q[plane, t * (E + 1)] = spread[E - 1 if t == 0 else 0] * masks[3 * s + 2 * t]
            acc[s * (E - 1)] += side([(q[plane, dy : dy + E], 6 * s + dy) for dy in range(3)])
        edge_wait(e)
        if e == 0:
            make_masks(2)
        for s in range(2):
            for t in range(2):
                edge = he_recv[e, 2 * s + t].astype(F32)[0:E]
                edge = x3(edge[None])[0] * masks[8 + 2 * s + t]
                q[s * (E + 1), t * (E + 1)] += edge
                acc[s * (E - 1), t * (E - 1)] += jnp.dot(
                    edge.astype(BF16), rows_of(w, 6 * s + 2 * t), preferred_element_type=F32
                )
        return acc[...].reshape(VOX, 128)

    def turn_weight(w_ref, wt):
        for t in range(13):
            wt[128 * t : 128 * t + 128, :] = dup_t(w_ref[:, 128 * t : 128 * t + 128].astype(F32)).astype(BF16)
        wt[1664:1728, :] = dup_t(w_ref[:, 1664:1728].astype(F32)).astype(BF16)
        wt[1728:1792, :] = jnp.zeros((64, 128), BF16)

    def flip_weight(w_ref, wf):
        low64 = lax.broadcasted_iota(jnp.int32, (64, 128), 1) < CH
        for t in range(13):
            tile = w_ref[:, 128 * t : 128 * t + 128].astype(F32)
            turned = pltpu.roll(tile, 64, 1)
            at = (26 - 2 * t) * 64
            wf[at : at + 64, :] = jnp.where(low64, tile, turned).astype(BF16)
            wf[at - 64 : at, :] = jnp.where(low64, turned, tile).astype(BF16)
        last = w_ref[:, 1664:1728].astype(F32)
        wf[0:64, :] = jnp.concatenate([last, last], axis=1).astype(BF16)
        wf[1728:1792, :] = jnp.zeros((64, 128), BF16)

    def terms(g, grads, q, ready):
        turned = grads.T[0:CH].astype(BF16)

        def put(t, tile):
            for r in range(4):
                t_send[g, 2 * r + t % 2, :, 128 * (t // 2) : 128 * (t // 2) + 128] = tile[
                    16 * r : 16 * r + 16
                ].astype(BF16)

        for m in range(5):
            even = jnp.dot(turned, patch(q, 2 * m), preferred_element_type=F32)
            put(3 * m, even[:, 0:128])
            if m == 4:
                put(3 * m + 1, even[:, 128:256])
            else:
                odd = jnp.dot(turned, patch(q, 2 * m + 1), preferred_element_type=F32)
                odd = pltpu.roll(odd, 64, 1)
                put(3 * m + 1, even[:, 128:256] + odd[:, 0:128])
                put(3 * m + 2, odd[:, 128:256])
            if m in ready:
                scatter_start(ready[m])

    def part_of(buffer, u, slot):
        g, lo, hi = UNITS[u]
        return buffer.at[g, slot, :, lo:hi]

    def t_copy(u, r):
        to = (mine + r) % members
        return pltpu.make_async_remote_copy(
            src_ref=part_of(t_send, u, to), dst_ref=part_of(t_recv, u, mine),
            send_sem=t_ss.at[u, r], recv_sem=t_rs.at[u, r],
            device_id=member_id(to), device_id_type=MESH,
        )

    def z_copy(u, r):
        return pltpu.make_async_remote_copy(
            src_ref=part_of(z_recv, u, group), dst_ref=part_of(z_recv, u, group),
            send_sem=z_ss.at[u, r], recv_sem=z_rs.at[u, r],
            device_id=group_id((group + r) % groups), device_id_type=MESH,
        )

    def g_copy(u, r):
        return pltpu.make_async_remote_copy(
            src_ref=part_of(gath, u, mine), dst_ref=part_of(gath, u, mine),
            send_sem=g_ss.at[u, r], recv_sem=g_rs.at[u, r],
            device_id=member_id((mine + r) % members), device_id_type=MESH,
        )

    def recv_of(buffer, u, slot, ss, rs, r):
        return pltpu.make_async_remote_copy(
            src_ref=part_of(buffer, u, slot), dst_ref=part_of(buffer, u, slot),
            send_sem=ss.at[u, r], recv_sem=rs.at[u, r],
            device_id=member_id((mine + 1) % members), device_id_type=MESH,
        )

    def add_up(buffer, u, count):
        g, lo, hi = UNITS[u]
        total = buffer[g, 0, :, lo:hi].astype(F32)
        for n in range(1, count):
            total = total + buffer[g, n, :, lo:hi].astype(F32)
        return total.astype(BF16)

    def scatter_start(u):
        g, lo, hi = UNITS[u]
        for r in range(1, members):
            t_copy(u, r).start()
        t_recv[g, mine, :, lo:hi] = t_send[g, mine, :, lo:hi]

    def exchange_start(u):
        g, lo, hi = UNITS[u]
        for r in range(1, members):
            recv_of(t_recv, u, (mine + members - r) % members, t_ss, t_rs, r).wait_recv()
        z_recv[g, group, :, lo:hi] = add_up(t_recv, u, members)
        for r in range(1, groups):
            z_copy(u, r).start()

    def gather_start(u):
        g, lo, hi = UNITS[u]
        for r in range(1, groups):
            recv_of(z_recv, u, (group + groups - r) % groups, z_ss, z_rs, r).wait_recv()
        gath[g, mine, :, lo:hi] = add_up(z_recv, u, groups)
        for r in range(1, members):
            g_copy(u, r).start()

    def gather_end(u, ref):
        g, lo, hi = UNITS[u]
        for r in range(1, members):
            recv_of(gath, u, (mine + members - r) % members, g_ss, g_rs, r).wait_recv()
        for r in range(4):
            for t in range(2 * lo // 128, 2 * hi // 128):
                end = min(128 * t + 128, 27 * CH)
                at = 128 * (t // 2)
                ref[16 * r : 16 * r + 16, 128 * t : end] = gath[
                    g, 2 * r + t % 2, :, at : at + end - 128 * t
                ]

    def reduce_done(u):
        for r in range(1, members):
            t_copy(u, r).wait_send()
            g_copy(u, r).wait_send()
        for r in range(1, groups):
            z_copy(u, r).wait_send()

    for q in (qx, qa, qg, qp):
        clear_halo(q)
    loads[0].wait()
    x = dup_t(x_ref[...].astype(F32))
    field = alive(x)
    fill_inside(qx, field)
    loads[1].wait()
    turn_weight(w1_ref, wt1)
    halo_send(0, field)
    conv_inside(qx, wt1)
    loads[2].wait()
    turn_weight(w2_ref, wt2)
    flip_weight(w2_ref, wf2)
    pre = conv_halo(0, qx, wt1)
    act = alive(pre * sigmoid(pre)).astype(BF16).astype(F32)

    halo_send(1, act)
    sig = sigmoid(pre)
    pre_s[...] = sig * (1.0 + pre * (1.0 - sig))
    fill_inside(qa, act)
    conv_inside(qa, wt2)
    flip_weight(w1_ref, wf1)
    loads[3].wait()
    ct = dup_t(ct_ref[...].astype(F32))
    summed = dup_t(x_ref[...].astype(F32)) + conv_halo(1, qa, wt2)
    sig = sigmoid(summed)
    gs = alive(ct * (sig * (1.0 + summed * (1.0 - sig)))).astype(BF16).astype(F32)

    halo_send(2, gs)
    gs_s[...] = gs
    terms(0, gs, qa, {4: 0})
    fill_inside(qg, gs)
    conv_inside(qg, wf2)
    out_ref[...] = alive(summed * sig).T[0:CH].astype(BF16)
    act_grad = conv_halo(2, qg, wf2)
    pg = alive(act_grad * pre_s[...]).astype(BF16).astype(F32)

    terms(1, pg, qx, {2: 1, 4: 2})
    halo_send(3, pg)
    exchange_start(0)
    fill_inside(qp, pg)
    conv_inside(qp, wf1)
    exchange_start(1)
    exchange_start(2)
    gather_start(0)
    gin = alive(gs_s[...] + conv_halo(3, qp, wf1))
    gather_start(1)
    gather_start(2)
    gin_ref[...] = gin.T[0:CH].astype(BF16)
    for e in range(4):
        sends_done(e)
    gather_end(0, g2_ref)
    gather_end(1, g1_ref)
    gather_end(2, g1_ref)
    for u in range(3):
        reduce_done(u)


def finish(scale, out_in, gin_in, g1_in, g2_in, out_ref, gin_ref, g1_ref, g2_ref):
    out_ref[...] = out_in[...]
    gin_ref[...] = gin_in[...]
    g1_ref[...] = g1_in[...].astype(F32) * scale
    g2_ref[...] = g2_in[...].astype(F32) * scale


def body(features, cotangent, first_weight, second_weight, positions, counts):
    n_gz = lax.axis_size("gz")
    n_gy = lax.axis_size("gy")
    slots = features.shape[2]
    scale = 1.0 / math.sqrt(n_gz * n_gy * slots * VOX)
    members = PAIR * n_gy
    groups = n_gz // PAIR
    vmem = pl.BlockSpec(memory_space=pltpu.VMEM)
    smem = pl.BlockSpec(memory_space=pltpu.SMEM)
    dma = pltpu.SemaphoreType.DMA
    hbm = pl.BlockSpec(memory_space=pl.ANY)
    output, input_grad, first_sum, second_sum = pl.pallas_call(
        functools.partial(kernel, n_gz, n_gy),
        out_shape=(
            pltpu.VMEM((CH, VOX), BF16),
            pltpu.VMEM((CH, VOX), BF16),
            pltpu.VMEM((CH, 27 * CH), BF16),
            pltpu.VMEM((CH, 27 * CH), BF16),
        ),
        in_specs=[smem, smem, hbm, hbm, hbm, hbm],
        out_specs=(vmem,) * 4,
        scratch_shapes=[
            pltpu.VMEM((CH, VOX), BF16),
            pltpu.VMEM((CH, VOX), BF16),
            pltpu.VMEM((CH, 27 * CH), BF16),
            pltpu.VMEM((CH, 27 * CH), BF16),
            dma((4,)),
            pltpu.VMEM((E + 2, E + 2, E, 256), F32),
            pltpu.VMEM((E + 2, E + 2, E, 256), F32),
            pltpu.VMEM((E + 2, E + 2, E, 256), F32),
            pltpu.VMEM((E + 2, E + 2, E, 256), F32),
            pltpu.VMEM((E, E, E, 128), F32),
            pltpu.VMEM((1792, 128), BF16),
            pltpu.VMEM((1792, 128), BF16),
            pltpu.VMEM((1792, 128), BF16),
            pltpu.VMEM((1792, 128), BF16),
            pltpu.VMEM((VOX, 128), F32),
            pltpu.VMEM((VOX, 128), F32),
            pltpu.VMEM((12, E, 256), F32),
            pltpu.VMEM((4, 4, 80, 128), BF16),
            pltpu.VMEM((4, 4, 80, 128), BF16),
            pltpu.VMEM((4, 4, 16, 128), BF16),
            pltpu.VMEM((4, 4, 16, 128), BF16),
            pltpu.VMEM((2, members, 16, 128 * TILES), BF16),
            pltpu.VMEM((2, members, 16, 128 * TILES), BF16),
            pltpu.VMEM((2, groups, 16, 128 * TILES), BF16),
            pltpu.VMEM((2, members, 16, 128 * TILES), BF16),
            dma((4, 4)), dma((4, 4)), dma((4, 4)), dma((4, 4)),
            dma((3, members)), dma((3, members)),
            dma((3, groups)), dma((3, groups)),
            dma((3, members)), dma((3, members)),
        ],
        compiler_params=pltpu.CompilerParams(collective_id=0, has_side_effects=True),
    )(
        positions.reshape(1), counts.reshape(1), features[0, 0, 0], cotangent[0, 0, 0],
        first_weight, second_weight,
    )
    grad = jax.ShapeDtypeStruct((CH, 27 * CH), F32)
    brick = jax.ShapeDtypeStruct((CH, VOX), BF16)
    output, input_grad, first_grad, second_grad = pl.pallas_call(
        functools.partial(finish, scale),
        out_shape=(brick, brick, grad, grad),
        in_specs=[vmem] * 4,
        out_specs=(vmem,) * 4,
    )(*(
        pltpu.with_memory_space_constraint(value, pltpu.VMEM)
        for value in (output, input_grad, first_sum, second_sum)
    ))
    return (output[None, None, None], input_grad[None, None, None], first_grad, second_grad)


def solution(mesh):
    return jax.shard_map(
        body,
        mesh=mesh,
        in_specs=(
            P("gz", "gy", None, None, None),
            P("gz", "gy", None, None, None),
            P(),
            P(),
            P("gz", "gy", None),
            P("gz", "gy"),
        ),
        out_specs=(P("gz", "gy", None, None, None), P("gz", "gy", None, None, None), P(), P()),
        check_vma=False,
    )
```
